256 devices in a mesh: seq: 16 (over y_hi, x, core), rep: 16 (over y_lo, z).
Axes of the slice: x: 4, y: 4 (y_hi: 2, y_lo: 2; y = y_hi * 2 + y_lo), z: 8, core: 2. Of those that a mesh axis runs over, the one named last changes fastest.
Arguments:
- query_rows: bfloat16 [32, 16, 256, 1152], P('rep', 'seq'), as said below
- key_rows: bfloat16 [32, 16, 256, 1152], P('rep', 'seq'), as said below
- value_rows: bfloat16 [32, 16, 256, 1152], P('rep', 'seq'), may hold values from -6 to 6
- out_grad: bfloat16 [32, 16, 256, 1152], P('rep', 'seq'), may hold values from -6 to 6
- out_weight: bfloat16 [1152, 1152], replicated, may hold values from -0.1875 to 0.1875
- frame_count: int32 [32], P('rep'), may hold values from 1 to 16, as said below
- pos_count: int32 [32], P('rep'), may hold values from 64 to 256, as said below
Outputs:
- projected: bfloat16 [32, 16, 256, 1152], P('rep', 'seq')
- grad_query: bfloat16 [32, 16, 256, 1152], P('rep', 'seq')
- grad_key: bfloat16 [32, 16, 256, 1152], P('rep', 'seq')
- grad_value: bfloat16 [32, 16, 256, 1152], P('rep', 'seq')
- grad_weight: float32 [1152, 1152], P('seq')
The draws below stay inside these ranges and needn't reach their ends.
Inputs may be any that keep to these rules, and one draw needn't show every extreme that they name: `query_rows`: entries lie within -40 to 40. `key_rows`: entries lie within -40 to 40. `frame_count`: some clip has all 16 frames live. `pos_count`: some clip has all 256 positions live.
All inputs are finite; a program needn't handle non-finite values.
Results may differ from the reference program's by a relative error of at most 0.0057.
Values may be sent and summed in bfloat16 or wider, within the bound.
A program may use at most 128 MiB of HBM per device.

```python
import math
import jax
import jax.numpy as jnp
from jax import lax

D = 1152
HEADS = 16
POS = 256
FRAMES = 16
CLIPS = 32


def query_key_pair(key):
    base = jax.random.fold_in(key, 7)
    key_query, key_keys = jax.random.split(base, 2)
    shape_all = (CLIPS, FRAMES, POS, D)
    query_drawn = jax.random.normal(key_query, shape_all, jnp.float32)
    keys_drawn = jax.random.normal(key_keys, shape_all, jnp.float32)
    return (query_drawn, keys_drawn)


def draw_query_rows(key, part):
    return query_key_pair(key)[0].astype(jnp.bfloat16)


def draw_key_rows(key, part):
    return query_key_pair(key)[1].astype(jnp.bfloat16)


def draw_frame_count(key, part):
    key_counts, key_pick = jax.random.split(jax.random.fold_in(key, 11))
    counts = jax.random.randint(key_counts, (CLIPS,), 1, FRAMES + 1)
    chosen = jax.random.randint(key_pick, (), 0, CLIPS)
    return jnp.where(jnp.arange(CLIPS) == chosen, FRAMES, counts).astype(jnp.int32)


def draw_pos_count(key, part):
    key_counts, key_pick = jax.random.split(jax.random.fold_in(key, 13))
    counts = jax.random.randint(key_counts, (CLIPS,), POS // 4, POS + 1)
    chosen = jax.random.randint(key_pick, (), 0, CLIPS)
    return jnp.where(jnp.arange(CLIPS) == chosen, POS, counts).astype(jnp.int32)


def strengthened(result, own_key, source, target, blocks, factor):
    owner, partner = [(jnp.arange(result.shape[dim]) // (result.shape[dim] // blocks)).reshape([-1 if axis == dim else 1 for axis in range(result.ndim)]) for dim in (source, target)]
    chosen = jax.random.permutation(own_key, blocks)[partner]
    strong = (owner == chosen) | (owner == (partner + blocks // 2) % blocks)
    return jnp.where(strong, factor * result, result)


def shard_levels(rng, extent, pieces, least, high):
    def one(axis_at, shards_of):
        steps = jax.random.uniform(jax.random.fold_in(jax.random.fold_in(rng, 6), axis_at), (shards_of,), jnp.float32, least / len(pieces), high / len(pieces))
        return jnp.repeat(jnp.exp(steps), extent[axis_at] // shards_of).reshape((-1,) + (1,) * (len(extent) - axis_at - 1))

    factor_of = one(*pieces[0])
    for cut in pieces[1:]:
        factor_of = factor_of * one(*cut)
    return factor_of


def bell_draw(stream_key, dims, scale, limit, cuts=(), held_as=jnp.bfloat16):
    loudness = shard_levels(stream_key, dims, cuts, -0.22, 0.18) if cuts else 1.0
    result = jax.random.normal(stream_key, dims, jnp.float32) * scale * loudness
    return jnp.minimum(jnp.maximum(result, -limit), limit).astype(held_as)


def gaussian_with(stream_key, extent, spread, most, cuts, heavy, kind=jnp.bfloat16):
    result = spread * jax.random.normal(stream_key, extent, jnp.float32)
    if cuts:
        result = result * shard_levels(stream_key, extent, cuts, -0.22, 0.18)
    return jnp.clip(strengthened(result, jax.random.fold_in(stream_key, 3), *heavy), -most, most).astype(kind)


def setup_inputs(seed: int = 0) -> dict:
    key_list = jax.random.split(jax.random.key(seed), 8)
    return {
        "query_rows": draw_query_rows(jax.random.fold_in(key_list[7], 71), 0),
        "key_rows": draw_key_rows(jax.random.fold_in(key_list[7], 71), 0),
        "value_rows": bell_draw(key_list[2], (CLIPS, FRAMES, POS, D), 1.0, 6.0, ((0, 16), (1, 16))),
        "out_grad": gaussian_with(key_list[3], (CLIPS, FRAMES, POS, D), 1.0, 6.0, ((0, 16), (1, 16)), (1, 3, 16, 2.0)),
        "out_weight": bell_draw(key_list[4], (D, D), D ** -0.5, 0.1875),
        "frame_count": draw_frame_count(jax.random.fold_in(key_list[7], 71), 0),
        "pos_count": draw_pos_count(jax.random.fold_in(key_list[7], 71), 0),
    }


def clip_pass(query_rows, key_rows, value_rows, out_grad, out_weight, frames_live, positions_live):
    nframe, npos_all, width = query_rows.shape
    head_dim = width // HEADS
    inv_root = 1.0 / math.sqrt(head_dim)
    shape_heads = (nframe, npos_all, HEADS, head_dim)
    query_heads = query_rows.astype(jnp.float32).reshape(shape_heads)
    key_heads = key_rows.astype(jnp.float32).reshape(shape_heads)
    value_heads = value_rows.astype(jnp.float32).reshape(shape_heads)
    scores = jnp.einsum('fphd,tphd->phft', query_heads, key_heads, precision=lax.Precision.HIGHEST) * inv_root
    frame_ids = jnp.arange(nframe, dtype=jnp.int32)
    key_live = frame_ids < frames_live
    scores = jnp.where(key_live, scores, -1e+30)
    highest = lax.optimization_barrier(jnp.max(scores, axis=-1, keepdims=True))
    expo = jnp.exp(scores - highest) * key_live.astype(jnp.float32)
    weights = expo / lax.optimization_barrier(jnp.sum(expo, axis=-1, keepdims=True))
    rounded = lax.optimization_barrier(weights.astype(jnp.bfloat16)).astype(jnp.float32)
    mixed = jnp.einsum('phft,tphd->fphd', rounded, value_heads, precision=lax.Precision.HIGHEST)
    row_live = key_live[:, None] & (jnp.arange(npos_all, dtype=jnp.int32) < positions_live)[None, :]
    attn_out = jnp.where(row_live[:, :, None], mixed.reshape(nframe, npos_all, width), 0.0).astype(jnp.bfloat16)
    flat_out = attn_out.reshape(-1, width)
    flat_grad = out_grad.reshape(-1, width)
    projected = jnp.dot(flat_out, out_weight.T, preferred_element_type=jnp.float32).astype(jnp.bfloat16)
    out_cot = jnp.dot(flat_grad, out_weight, preferred_element_type=jnp.float32).reshape(nframe, npos_all, width)
    out_cot = jnp.where(row_live[:, :, None], out_cot, 0.0).astype(jnp.bfloat16)
    weight_term = lax.dot_general(flat_grad, flat_out, (((0,), (0,)), ((), ())), preferred_element_type=jnp.float32)
    cot_heads = out_cot.astype(jnp.float32).reshape(shape_heads)
    grad_value = jnp.einsum('phft,fphd->tphd', rounded, cot_heads, precision=lax.Precision.HIGHEST)
    grad_attn = jnp.einsum('fphd,tphd->phft', cot_heads, value_heads, precision=lax.Precision.HIGHEST)
    row_delta = lax.optimization_barrier(jnp.sum(weights * grad_attn, axis=-1, keepdims=True))
    grad_score = weights * (grad_attn - row_delta) * inv_root
    grad_query = jnp.einsum('phft,tphd->fphd', grad_score, key_heads, precision=lax.Precision.HIGHEST)
    grad_key = jnp.einsum('phft,fphd->tphd', grad_score, query_heads, precision=lax.Precision.HIGHEST)
    full = (nframe, npos_all, width)
    return (projected.reshape(full), grad_query.reshape(full).astype(jnp.bfloat16), grad_key.reshape(full).astype(jnp.bfloat16), grad_value.reshape(full).astype(jnp.bfloat16), weight_term)

def reference(query_rows, key_rows, value_rows, out_grad, out_weight, frame_count, pos_count):

    def advance(total, items):
        results = clip_pass(items[0], items[1], items[2], items[3], out_weight, items[4], items[5])
        return (total + results[4], results[:4])
    start_total = jnp.zeros((D, D), jnp.float32)
    total, stacked = lax.scan(advance, start_total, (query_rows, key_rows, value_rows, out_grad, frame_count, pos_count))
    return (stacked[0], stacked[1], stacked[2], stacked[3], total)
```

```python
import functools
import math

import jax
import jax.numpy as jnp
from jax import lax
from jax.experimental import pallas as pl
from jax.experimental.pallas import tpu as pltpu
from jax.sharding import PartitionSpec as P

HEADS = 16
MESH = pl.DeviceIdType.MESH
VMEM_BYTES = 56 << 20


def greet(n):
    me = lax.axis_index("seq")
    barrier = pltpu.get_barrier_semaphore()

    def signal(j, carry):
        pl.semaphore_signal(
            barrier, inc=1, device_id={"seq": lax.rem(me + j, n)}, device_id_type=MESH
        )
        return carry

    lax.fori_loop(1, n, signal, 0)
    pl.semaphore_wait(barrier, n - 1)
    return me


def to_positions_kernel(n, *refs):
    sources, targets = refs[:4], refs[4:8]
    send, recv, local = refs[8:]
    me = greet(n)
    clips, part = targets[0].shape[0], targets[0].shape[2]
    own = []
    for c in range(clips):
        for a in range(4):
            mine = pl.ds(pl.multiple_of(me * part, part), part)
            copy = pltpu.make_async_copy(
                sources[a].at[c, 0, mine], targets[a].at[c, me], local.at[c, a]
            )
            copy.start()
            own.append(copy)

            def push(j, carry):
                peer = lax.rem(me + j, n)
                theirs = pl.ds(pl.multiple_of(peer * part, part), part)
                pltpu.make_async_remote_copy(
                    src_ref=sources[a].at[c, 0, theirs],
                    dst_ref=targets[a].at[c, me],
                    send_sem=send.at[c, a],
                    recv_sem=recv.at[c, a],
                    device_id={"seq": peer},
                    device_id_type=MESH,
                ).start()
                return carry

            lax.fori_loop(1, n, push, 0)
    for copy in own:
        copy.wait()
    for c in range(clips):
        for a in range(4):
            whole = targets[a].at[c, pl.ds(0, n - 1)]
            pltpu.make_async_copy(whole, whole, recv.at[c, a]).wait()
            pltpu.make_async_copy(whole, whole, send.at[c, a]).wait()


def to_frames_kernel(n, *refs):
    sources, targets = refs[:4], refs[4:8]
    send, recv, local = refs[8:]
    me = greet(n)
    clips, part = sources[0].shape[0], sources[0].shape[2]
    mine = pl.ds(pl.multiple_of(me * part, part), part)
    own = []
    for c in range(clips):
        for a in range(4):
            copy = pltpu.make_async_copy(
                sources[a].at[c, me], targets[a].at[c, 0, mine], local.at[c, a]
            )
            copy.start()
            own.append(copy)

            def push(j, carry):
                peer = lax.rem(me + j, n)
                pltpu.make_async_remote_copy(
                    src_ref=sources[a].at[c, peer],
                    dst_ref=targets[a].at[c, 0, mine],
                    send_sem=send.at[c, a],
                    recv_sem=recv.at[c, a],
                    device_id={"seq": peer},
                    device_id_type=MESH,
                ).start()
                return carry

            lax.fori_loop(1, n, push, 0)
    for copy in own:
        copy.wait()
    for c in range(clips):
        for a in range(4):
            whole = sources[a].at[c, pl.ds(0, n - 1)]
            pltpu.make_async_copy(whole, whole, recv.at[c, a]).wait()
            pltpu.make_async_copy(whole, whole, send.at[c, a]).wait()


def exchange(kernel, n, arrays, out_shape, collective_id):
    clips = arrays[0].shape[0]
    return pl.pallas_call(
        functools.partial(kernel, n),
        out_shape=[jax.ShapeDtypeStruct(out_shape, jnp.bfloat16)] * 4,
        in_specs=[pl.BlockSpec(memory_space=pl.ANY)] * 4,
        out_specs=[pl.BlockSpec(memory_space=pl.ANY)] * 4,
        scratch_shapes=[pltpu.SemaphoreType.DMA((clips, 4))] * 3,
        compiler_params=pltpu.CompilerParams(collective_id=collective_id, has_side_effects=True),
    )(*arrays)


def columns_of(width):
    step = 384 if width % 384 == 0 else width
    return [pl.ds(i, step) for i in range(0, width, step)]


def attend(part, place, frames, places, query, key, value, grad, weight, cot, attn, bias, outs):
    projected, grad_query, grad_key, grad_value = outs
    rows, width = query.shape
    head_dim = width // HEADS
    inv_root = 1.0 / math.sqrt(head_dim)
    row = lax.broadcasted_iota(jnp.int32, (rows, 1), 0)
    live = (row // part < frames) & (place + row % part < places)
    for cols in columns_of(width):
        wide = jnp.dot(grad[...], weight[:, cols], preferred_element_type=jnp.float32)
        cot[:, cols] = jnp.where(live, wide, 0.0).astype(jnp.bfloat16)
    key_row = lax.broadcasted_iota(jnp.int32, (rows, rows), 0)
    query_row = lax.broadcasted_iota(jnp.int32, (rows, rows), 1)
    allowed = (key_row % part == query_row % part) & (key_row // part < frames)
    bias[...] = jnp.where(allowed, 0.0, -1e30)

    def head(h, carry):
        low = jnp.minimum((h * head_dim) // 128 * 128, width - 256)
        window = pl.ds(pl.multiple_of(low, 128), 256)
        lane = lax.broadcasted_iota(jnp.int32, (rows, 256), 1) + low
        inside = (lane >= h * head_dim) & (lane < (h + 1) * head_dim)
        zero = jnp.zeros((rows, 256), jnp.bfloat16)
        key_h, value_h = key[:, window], value[:, window]
        query_h = jnp.where(inside, query[:, window], zero)
        cot_h = jnp.where(inside, cot[:, window], zero)
        scores = lax.dot_general(
            key_h, query_h, (((1,), (1,)), ((), ())), preferred_element_type=jnp.float32
        )
        scores = scores + bias[...]
        highest = jnp.max(scores, axis=0, keepdims=True)
        expo = jnp.exp2((scores - highest) * (inv_root * math.log2(math.e)))
        weights = expo * (1.0 / jnp.sum(expo, axis=0, keepdims=True))
        rounded = weights.astype(jnp.bfloat16)
        mixed = lax.dot_general(
            rounded, value_h, (((0,), (0,)), ((), ())), preferred_element_type=jnp.float32
        )
        mixed = jnp.where(live, mixed, 0.0).astype(jnp.bfloat16)
        attn[:, window] = jnp.where(inside, mixed, attn[:, window])
        gv = jnp.dot(rounded, cot_h, preferred_element_type=jnp.float32).astype(jnp.bfloat16)
        grad_value[:, window] = jnp.where(inside, gv, grad_value[:, window])
        grad_attn = lax.dot_general(
            value_h, cot_h, (((1,), (1,)), ((), ())), preferred_element_type=jnp.float32
        )
        delta = jnp.sum(weights * grad_attn, axis=0, keepdims=True)
        grad_score = (weights * (grad_attn - delta) * inv_root).astype(jnp.bfloat16)
        gq = lax.dot_general(
            grad_score, key_h, (((0,), (0,)), ((), ())), preferred_element_type=jnp.float32
        ).astype(jnp.bfloat16)
        grad_query[:, window] = jnp.where(inside, gq, grad_query[:, window])
        gk = jnp.dot(grad_score, query_h, preferred_element_type=jnp.float32).astype(jnp.bfloat16)
        grad_key[:, window] = jnp.where(inside, gk, grad_key[:, window])
        return carry

    lax.fori_loop(0, HEADS, head, 0)
    for cols in columns_of(width):
        projected[:, cols] = lax.dot_general(
            attn[...], weight[cols, :], (((1,), (1,)), ((), ())), preferred_element_type=jnp.float32
        ).astype(jnp.bfloat16)


def compute_kernel(part, frames, places, query, key, value, grad, weight, *refs):
    outs, total, (cot, attn, bias) = refs[:4], refs[4], refs[5:]
    c = pl.program_id(0)
    place = lax.axis_index("seq") * part
    squeeze = [r.at[0] for r in (query, key, value, grad)]
    attend(
        part, place, frames[c], places[c], *squeeze, weight, cot, attn, bias,
        [r.at[0] for r in outs],
    )

    @pl.when(c == 0)
    def _():
        total[...] = jnp.zeros_like(total)

    for rows in columns_of(total.shape[0]):
        total[rows, :] += lax.dot_general(
            grad[0, :, rows], attn[...], (((0,), (0,)), ((), ())),
            preferred_element_type=jnp.float32,
        )


def compute(arrays, weight, frames, places, part):
    clips, rows, width = arrays[0].shape
    block = pl.BlockSpec((1, rows, width), lambda c: (c, 0, 0))
    fixed = pl.BlockSpec((width, width), lambda c: (0, 0))
    smem = pl.BlockSpec(memory_space=pltpu.SMEM)
    shape = jax.ShapeDtypeStruct((clips, rows, width), jnp.bfloat16)
    return pl.pallas_call(
        functools.partial(compute_kernel, part),
        grid=(clips,),
        out_shape=[shape] * 4 + [jax.ShapeDtypeStruct((width, width), jnp.float32)],
        in_specs=[smem, smem] + [block] * 4 + [fixed],
        out_specs=[block] * 4 + [fixed],
        scratch_shapes=[
            pltpu.VMEM((rows, width), jnp.bfloat16),
            pltpu.VMEM((rows, width), jnp.bfloat16),
            pltpu.VMEM((rows, rows), jnp.float32),
        ],
        compiler_params=pltpu.CompilerParams(vmem_limit_bytes=VMEM_BYTES),
    )(frames, places, *arrays, weight)


def shards(query_rows, key_rows, value_rows, out_grad, out_weight, frame_count, pos_count):
    clips, _, places, width = query_rows.shape
    n = lax.axis_size("seq")
    part = places // n
    moved = exchange(
        to_positions_kernel,
        n,
        (query_rows, key_rows, value_rows, out_grad),
        (clips, n, part, width),
        0,
    )
    moved = [m.reshape(clips, n * part, width) for m in moved]
    *results, partial_term = compute(moved, out_weight, frame_count, pos_count, part)
    results = [r.reshape(clips, n, part, width) for r in results]
    grad_weight = lax.psum_scatter(partial_term, "seq", scatter_dimension=0, tiled=True)
    grad_weight = lax.psum(grad_weight, "rep")
    back = exchange(to_frames_kernel, n, results, (clips, 1, places, width), 1)
    return (*back, grad_weight)


def solution(mesh):
    rows = P("rep", "seq", None, None)
    return jax.shard_map(
        shards,
        mesh=mesh,
        in_specs=(rows, rows, rows, rows, P(), P("rep"), P("rep")),
        out_specs=(rows, rows, rows, rows, P("seq", None)),
        check_vma=False,
    )
```

```python
import functools
import math

import jax
import jax.numpy as jnp
from jax import lax
from jax.experimental import pallas as pl
from jax.experimental.pallas import tpu as pltpu
from jax.sharding import PartitionSpec as P

HEADS = 16
RING = 8
SLABS = 9
MESH = pl.DeviceIdType.MESH
VMEM_BYTES = 56 << 20


def greet(peers):
    barrier = pltpu.get_barrier_semaphore()
    for first, count, peer_of in peers:

        def signal(j, carry):
            pl.semaphore_signal(barrier, inc=1, device_id=peer_of(j), device_id_type=MESH)
            return carry

        lax.fori_loop(first, first + count, signal, 0)
    pl.semaphore_wait(barrier, sum(count for _, count, _ in peers))


def row_peers(n):
    s, r = lax.axis_index("seq"), lax.axis_index("rep")
    return (1, n - 1, lambda j: (lax.rem(s + j, n), r))


def to_positions_kernel(n, *refs):
    sources, targets = refs[:4], refs[4:8]
    send, recv, local = refs[8:]
    me = lax.axis_index("seq")
    greet([row_peers(n)])
    clips, part = targets[0].shape[0], targets[0].shape[2]
    own = []
    for c in range(clips):
        for a in range(4):
            mine = pl.ds(pl.multiple_of(me * part, part), part)
            copy = pltpu.make_async_copy(
                sources[a].at[c, 0, mine], targets[a].at[c, me], local.at[c, a]
            )
            copy.start()
            own.append(copy)

            def push(j, carry):
                peer = lax.rem(me + j, n)
                theirs = pl.ds(pl.multiple_of(peer * part, part), part)
                pltpu.make_async_remote_copy(
                    src_ref=sources[a].at[c, 0, theirs],
                    dst_ref=targets[a].at[c, me],
                    send_sem=send.at[c, a],
                    recv_sem=recv.at[c, a],
                    device_id={"seq": peer},
                    device_id_type=MESH,
                ).start()
                return carry

            lax.fori_loop(1, n, push, 0)
    for copy in own:
        copy.wait()
    for c in range(clips):
        for a in range(4):
            whole = targets[a].at[c, pl.ds(0, n - 1)]
            pltpu.make_async_copy(whole, whole, recv.at[c, a]).wait()
            pltpu.make_async_copy(whole, whole, send.at[c, a]).wait()


def slab_place(slab):
    block, i = slab // SLABS, slab % SLABS
    core, chip = block % 2, block // 2
    return (core, i, chip) if i < RING else (core, chip, RING)


class WeightSum:
    def __init__(self, term, out, half, ring, plane, last, sems):
        self.term, self.out, self.half, self.ring, self.plane, self.last = (
            term, out, half, ring, plane, last,
        )
        (self.half_sems, self.ring_send, self.ring_recv, self.plane_sems, self.z_sems) = sems
        self.s, self.r = lax.axis_index("seq"), lax.axis_index("rep")
        self.core, self.chip = lax.rem(self.s, 2), lax.div(self.s, 2)
        self.z, self.low = lax.rem(self.r, RING), lax.div(self.r, RING)

    def peers(self):
        s, r, core, z, low = self.s, self.r, self.core, self.z, self.low
        return [
            (0, RING, lambda j: (2 * j + core, (1 - low) * RING + z)),
            (1, RING - 1, lambda j: (s, low * RING + lax.rem(z + j, RING))),
        ]

    def half_copy(self):
        return pltpu.make_async_remote_copy(
            src_ref=self.term.at[1 - self.core],
            dst_ref=self.half,
            send_sem=self.half_sems.at[0],
            recv_sem=self.half_sems.at[1],
            device_id=(self.s + 1 - 2 * self.core, self.r),
            device_id_type=MESH,
        )

    def add_half(self):
        self.half_copy().wait()

        def add(j, carry):
            self.half[j] += self.term[self.core, j]
            return carry

        lax.fori_loop(0, RING, add, 0)

    def piece(self, t):
        way = 1 - 2 * self.core
        return lax.rem(self.z - way * (t + 1) + 2 * RING, RING)

    def ring_copy(self, t):
        way = 1 - 2 * self.core
        return pltpu.make_async_remote_copy(
            src_ref=self.half.at[self.piece(0)] if t == 0 else self.ring.at[t - 1],
            dst_ref=self.ring.at[t],
            send_sem=self.ring_send.at[t],
            recv_sem=self.ring_recv.at[t],
            device_id=(self.s, self.low * RING + lax.rem(self.z + way + RING, RING)),
            device_id_type=MESH,
        )

    def ring_step(self, t):
        self.ring_copy(t).wait_recv()
        self.ring[t] += self.half[self.piece(t + 1)]
        if t + 1 < RING - 1:
            self.ring_copy(t + 1).start()

    def spread(self, start):
        held, me = self.ring.at[RING - 2], self.low * RING + self.chip

        def each(j, carry):
            chip, low = lax.rem(j, RING), lax.div(j, RING)
            self.plane_copy(held.at[chip], self.plane.at[0, me], 0, 2 * chip + self.core, low, start)
            return carry

        lax.fori_loop(0, 2 * RING, each, 0)
        for low in range(2):
            self.plane_copy(held.at[RING], self.plane.at[1, me], 1, 2 * self.z + self.core, low, start)

    def plane_copy(self, src, dst, k, s, low, start):
        is_self = (s == self.s) & (low == self.low)

        @pl.when(jnp.logical_not(is_self))
        def _():
            copy = pltpu.make_async_remote_copy(
                src_ref=src,
                dst_ref=dst,
                send_sem=self.plane_sems.at[0, k],
                recv_sem=self.plane_sems.at[1, k],
                device_id=(s, low * RING + self.z),
                device_id_type=MESH,
            )
            if start:
                copy.start()
            else:
                copy.wait_send()

        if start:

            @pl.when(is_self)
            def _():
                self.plane[k, self.low * RING + self.chip] = self.ring[
                    RING - 2, self.chip if k == 0 else RING
                ]

    def z_copy(self, k, j):
        rows = pl.ds(pl.multiple_of(self.z * 8, 8) if k == 0 else RING * 8, 8)
        return pltpu.make_async_remote_copy(
            src_ref=self.last.at[k],
            dst_ref=self.out.at[rows],
            send_sem=self.z_sems.at[0, k],
            recv_sem=self.z_sems.at[1, k],
            device_id=(self.s, self.low * RING + lax.rem(self.z + j, RING)),
            device_id_type=MESH,
        )

    def to_all_z(self, k, start):
        def each(j, carry):
            copy = self.z_copy(k, j)
            if start:
                copy.start()
            else:
                copy.wait_send()
            return carry

        lax.fori_loop(1, RING, each, 0)

    def gather(self):
        for k in range(2):

            @pl.when((self.chip == self.z) | (k == 0))
            def _():
                whole = self.plane.at[k, pl.ds(0, 2 * RING - 1)]
                pltpu.make_async_copy(whole, whole, self.plane_sems.at[1, k]).wait()
                total = self.plane[k, 0]
                for i in range(1, 2 * RING):
                    total = total + self.plane[k, i]
                self.last[k] = total
                self.to_all_z(k, True)
                rows = pl.ds(pl.multiple_of(self.z * 8, 8) if k == 0 else RING * 8, 8)
                self.out[rows] = total

    def finish(self):
        whole = self.plane.at[0, pl.ds(0, RING - 1)]
        pltpu.make_async_copy(whole, whole, self.z_sems.at[1, 0]).wait()
        self.to_all_z(0, False)

        @pl.when(self.chip == self.z)
        def _():
            self.to_all_z(1, False)

        @pl.when(self.chip != self.z)
        def _():
            one = self.plane.at[1, 0]
            pltpu.make_async_copy(one, one, self.z_sems.at[1, 1]).wait()

        self.spread(False)
        for t in range(RING - 1):
            self.ring_copy(t).wait_send()


def to_frames_kernel(n, *refs):
    sources, term, targets, out = refs[:4], refs[4], refs[5:9], refs[9]
    half, ring, plane, last, send, recv, local = refs[10:17]
    weight_sum = WeightSum(term, out, half, ring, plane, last, refs[17:])
    me = lax.axis_index("seq")
    rep = lax.axis_index("rep")
    greet([row_peers(n)] + weight_sum.peers())
    clips, part = sources[0].shape[0], sources[0].shape[2]
    mine = pl.ds(pl.multiple_of(me * part, part), part)
    own = []

    def post(c, a):
        copy = pltpu.make_async_copy(
            sources[a].at[c, me], targets[a].at[c, 0, mine], local.at[c, a]
        )
        copy.start()
        own.append(copy)

        def push(j, carry):
            peer = lax.rem(me + j, n)
            pltpu.make_async_remote_copy(
                src_ref=sources[a].at[c, peer],
                dst_ref=targets[a].at[c, 0, mine],
                send_sem=send.at[c, a],
                recv_sem=recv.at[c, a],
                device_id=(peer, rep),
                device_id_type=MESH,
            ).start()
            return carry

        lax.fori_loop(1, n, push, 0)

    weight_sum.half_copy().start()
    post(0, 0)
    weight_sum.add_half()
    weight_sum.ring_copy(0).start()
    posts = [(c, a) for c in range(clips) for a in range(4)][1:]
    for t in range(RING - 1):
        post(*posts[t])
        weight_sum.ring_step(t)
    weight_sum.spread(True)
    weight_sum.gather()
    weight_sum.finish()
    for copy in own:
        copy.wait()
    for c in range(clips):
        for a in range(4):
            whole = sources[a].at[c, pl.ds(0, n - 1)]
            pltpu.make_async_copy(whole, whole, recv.at[c, a]).wait()
            pltpu.make_async_copy(whole, whole, send.at[c, a]).wait()


def to_positions(n, arrays, out_shape):
    clips = arrays[0].shape[0]
    return pl.pallas_call(
        functools.partial(to_positions_kernel, n),
        out_shape=[jax.ShapeDtypeStruct(out_shape, jnp.bfloat16)] * 4,
        in_specs=[pl.BlockSpec(memory_space=pl.ANY)] * 4,
        out_specs=[pl.BlockSpec(memory_space=pl.ANY)] * 4,
        scratch_shapes=[pltpu.SemaphoreType.DMA((clips, 4))] * 3,
        compiler_params=pltpu.CompilerParams(collective_id=0, has_side_effects=True),
    )(*arrays)


def to_frames(n, arrays, term, out_shape):
    clips, width = arrays[0].shape[0], term.shape[-1]
    dma = pltpu.SemaphoreType.DMA
    return pl.pallas_call(
        functools.partial(to_frames_kernel, n),
        out_shape=[jax.ShapeDtypeStruct(out_shape, jnp.bfloat16)] * 4
        + [jax.ShapeDtypeStruct((SLABS * 8, width), jnp.float32)],
        in_specs=[pl.BlockSpec(memory_space=pl.ANY)] * 4 + [pl.BlockSpec(memory_space=pltpu.VMEM)],
        out_specs=[pl.BlockSpec(memory_space=pl.ANY)] * 4
        + [pl.BlockSpec(memory_space=pltpu.VMEM)],
        scratch_shapes=[
            pltpu.VMEM((RING, SLABS, 8, width), jnp.float32),
            pltpu.VMEM((RING - 1, SLABS, 8, width), jnp.float32),
            pltpu.VMEM((2, 2 * RING, 8, width), jnp.float32),
            pltpu.VMEM((2, 8, width), jnp.float32),
            dma((clips, 4)),
            dma((clips, 4)),
            dma((clips, 4)),
            dma((2,)),
            dma((RING - 1,)),
            dma((RING - 1,)),
            dma((2, 2)),
            dma((2, 2)),
        ],
        compiler_params=pltpu.CompilerParams(
            collective_id=1, has_side_effects=True, vmem_limit_bytes=VMEM_BYTES
        ),
    )(*arrays, term)


def columns_of(width):
    step = 384 if width % 384 == 0 else width
    return [pl.ds(i, step) for i in range(0, width, step)]


def attend(part, place, frames, places, query, key, value, grad, weight, cot, attn, bias, outs):
    projected, grad_query, grad_key, grad_value = outs
    rows, width = query.shape
    head_dim = width // HEADS
    inv_root = 1.0 / math.sqrt(head_dim)
    row = lax.broadcasted_iota(jnp.int32, (rows, 1), 0)
    live = (row // part < frames) & (place + row % part < places)
    for cols in columns_of(width):
        wide = jnp.dot(grad[...], weight[:, cols], preferred_element_type=jnp.float32)
        cot[:, cols] = jnp.where(live, wide, 0.0).astype(jnp.bfloat16)
    key_row = lax.broadcasted_iota(jnp.int32, (rows, rows), 0)
    query_row = lax.broadcasted_iota(jnp.int32, (rows, rows), 1)
    allowed = (key_row % part == query_row % part) & (key_row // part < frames)
    bias[...] = jnp.where(allowed, 0.0, -1e30)

    def head(h, carry):
        low = jnp.minimum((h * head_dim) // 128 * 128, width - 256)
        window = pl.ds(pl.multiple_of(low, 128), 256)
        lane = lax.broadcasted_iota(jnp.int32, (rows, 256), 1) + low
        inside = (lane >= h * head_dim) & (lane < (h + 1) * head_dim)
        zero = jnp.zeros((rows, 256), jnp.bfloat16)
        key_h, value_h = key[:, window], value[:, window]
        query_h = jnp.where(inside, query[:, window], zero)
        cot_h = jnp.where(inside, cot[:, window], zero)
        scores = lax.dot_general(
            key_h, query_h, (((1,), (1,)), ((), ())), preferred_element_type=jnp.float32
        )
        scores = scores + bias[...]
        highest = jnp.max(scores, axis=0, keepdims=True)
        expo = jnp.exp2((scores - highest) * (inv_root * math.log2(math.e)))
        weights = expo * (1.0 / jnp.sum(expo, axis=0, keepdims=True))
        rounded = weights.astype(jnp.bfloat16)
        mixed = lax.dot_general(
            rounded, value_h, (((0,), (0,)), ((), ())), preferred_element_type=jnp.float32
        )
        mixed = jnp.where(live, mixed, 0.0).astype(jnp.bfloat16)
        attn[:, window] = jnp.where(inside, mixed, attn[:, window])
        gv = jnp.dot(rounded, cot_h, preferred_element_type=jnp.float32).astype(jnp.bfloat16)
        grad_value[:, window] = jnp.where(inside, gv, grad_value[:, window])
        grad_attn = lax.dot_general(
            value_h, cot_h, (((1,), (1,)), ((), ())), preferred_element_type=jnp.float32
        )
        delta = jnp.sum(weights * grad_attn, axis=0, keepdims=True)
        grad_score = (weights * (grad_attn - delta) * inv_root).astype(jnp.bfloat16)
        gq = lax.dot_general(
            grad_score, key_h, (((0,), (0,)), ((), ())), preferred_element_type=jnp.float32
        ).astype(jnp.bfloat16)
        grad_query[:, window] = jnp.where(inside, gq, grad_query[:, window])
        gk = jnp.dot(grad_score, query_h, preferred_element_type=jnp.float32).astype(jnp.bfloat16)
        grad_key[:, window] = jnp.where(inside, gk, grad_key[:, window])
        return carry

    lax.fori_loop(0, HEADS, head, 0)
    for cols in columns_of(width):
        projected[:, cols] = lax.dot_general(
            attn[...], weight[cols, :], (((1,), (1,)), ((), ())), preferred_element_type=jnp.float32
        ).astype(jnp.bfloat16)


def weight_term(grad, attn, term):
    for rows in columns_of(grad.shape[1]):
        found = lax.dot_general(
            grad[:, rows], attn[...], (((0,), (0,)), ((), ())), preferred_element_type=jnp.float32
        )
        for k in range(rows.size // 8):
            term[slab_place(rows.start // 8 + k)] = found[8 * k : 8 * k + 8]


def compute_kernel(part, frames, places, query, key, value, grad, weight, *refs):
    outs, term, (cot, attn, bias) = refs[:4], refs[4], refs[5:]
    c = pl.program_id(0)
    place = lax.axis_index("seq") * part
    rows = query.shape[1]
    mine = pl.ds(pl.multiple_of(c * rows, rows), rows)
    attend(
        part, place, frames[c], places[c],
        query.at[0], key.at[0], value.at[0], grad.at[mine],
        weight, cot, attn.at[mine], bias, [r.at[0] for r in outs],
    )

    @pl.when(c == pl.num_programs(0) - 1)
    def _():
        weight_term(grad, attn, term)


def compute(arrays, weight, frames, places, part):
    clips, rows, width = arrays[0].shape
    block = pl.BlockSpec((1, rows, width), lambda c: (c, 0, 0))

    def fixed(*shape):
        return pl.BlockSpec(shape, lambda c: (0,) * len(shape))

    smem = pl.BlockSpec(memory_space=pltpu.SMEM)
    shape = jax.ShapeDtypeStruct((clips, rows, width), jnp.bfloat16)
    term_shape = (2, RING, SLABS, 8, width)
    query, key, value, grad = arrays
    return pl.pallas_call(
        functools.partial(compute_kernel, part),
        grid=(clips,),
        out_shape=[shape] * 4 + [jax.ShapeDtypeStruct(term_shape, jnp.float32)],
        in_specs=[smem, smem] + [block] * 3 + [fixed(clips * rows, width), fixed(width, width)],
        out_specs=[block] * 4 + [fixed(*term_shape)],
        scratch_shapes=[
            pltpu.VMEM((rows, width), jnp.bfloat16),
            pltpu.VMEM((clips * rows, width), jnp.bfloat16),
            pltpu.VMEM((rows, rows), jnp.float32),
        ],
        compiler_params=pltpu.CompilerParams(vmem_limit_bytes=VMEM_BYTES),
    )(frames, places, query, key, value, grad.reshape(clips * rows, width), weight)


def shards(query_rows, key_rows, value_rows, out_grad, out_weight, frame_count, pos_count):
    clips, _, places, width = query_rows.shape
    n = lax.axis_size("seq")
    part = places // n
    moved = to_positions(
        n, (query_rows, key_rows, value_rows, out_grad), (clips, n, part, width)
    )
    moved = [m.reshape(clips, n * part, width) for m in moved]
    *results, term = compute(moved, out_weight, frame_count, pos_count, part)
    results = [r.reshape(clips, n, part, width) for r in results]
    return tuple(to_frames(n, results, term, (clips, 1, places, width)))


def solution(mesh):
    rows = P("rep", "seq", None, None)
    return jax.shard_map(
        shards,
        mesh=mesh,
        in_specs=(rows, rows, rows, rows, P(), P("rep"), P("rep")),
        out_specs=(rows, rows, rows, rows, P("seq", None)),
        check_vma=False,
    )
```

```python
import functools
import math

import jax
import jax.numpy as jnp
from jax import lax
from jax.experimental import pallas as pl
from jax.experimental.pallas import tpu as pltpu
from jax.sharding import PartitionSpec as P

HEADS = 16
RING = 8
SLABS = 9
TOGETHER = 4
SUB = 3
MESH = pl.DeviceIdType.MESH
VMEM_BYTES = 56 << 20


def greet(peers):
    barrier = pltpu.get_barrier_semaphore()
    for first, count, peer_of in peers:

        def signal(j, carry):
            pl.semaphore_signal(barrier, inc=1, device_id=peer_of(j), device_id_type=MESH)
            return carry

        lax.fori_loop(first, first + count, signal, 0)
    pl.semaphore_wait(barrier, sum(count for _, count, _ in peers))


def row_peers(n):
    s, r = lax.axis_index("seq"), lax.axis_index("rep")
    return (1, n - 1, lambda j: (lax.rem(s + j, n), r))


def slab_place(slab):
    block, i = slab // SLABS, slab % SLABS
    core, chip = block % 2, block // 2
    return (core, i, chip) if i < RING else (core, chip, RING)


class WeightSum:
    def __init__(self, term, out, half, ring, plane, last, sems):
        self.term, self.out, self.half, self.ring, self.plane, self.last = (
            term, out, half, ring, plane, last,
        )
        (self.half_sems, self.ring_send, self.ring_recv, self.plane_sems, self.z_sems) = sems
        self.s, self.r = lax.axis_index("seq"), lax.axis_index("rep")
        self.core, self.chip = lax.rem(self.s, 2), lax.div(self.s, 2)
        self.z, self.low = lax.rem(self.r, RING), lax.div(self.r, RING)

    def peers(self):
        s, r, core, z, low = self.s, self.r, self.core, self.z, self.low
        return [
            (0, RING, lambda j: (2 * j + core, (1 - low) * RING + z)),
            (1, RING - 1, lambda j: (s, low * RING + lax.rem(z + j, RING))),
        ]

    def half_copy(self):
        return pltpu.make_async_remote_copy(
            src_ref=self.term.at[1 - self.core],
            dst_ref=self.half,
            send_sem=self.half_sems.at[0],
            recv_sem=self.half_sems.at[1],
            device_id=(self.s + 1 - 2 * self.core, self.r),
            device_id_type=MESH,
        )

    def add_half(self):
        self.half_copy().wait()

        def add(j, carry):
            self.half[j] += self.term[self.core, j]
            return carry

        lax.fori_loop(0, RING, add, 0)

    def piece(self, t):
        way = 1 - 2 * self.core
        return lax.rem(self.z - way * (t + 1) + 2 * RING, RING)

    def ring_copy(self, t, u):
        way = 1 - 2 * self.core
        slots = pl.ds(u * SUB, SUB)
        return pltpu.make_async_remote_copy(
            src_ref=self.half.at[self.piece(0), slots] if t == 0 else self.ring.at[t - 1, slots],
            dst_ref=self.ring.at[t, slots],
            send_sem=self.ring_send.at[t, u],
            recv_sem=self.ring_recv.at[t, u],
            device_id=(self.s, self.low * RING + lax.rem(self.z + way + RING, RING)),
            device_id_type=MESH,
        )

    def ring_start(self):
        for u in range(SLABS // SUB):
            self.ring_copy(0, u).start()

    def ring_step(self, t):
        for u in range(SLABS // SUB):
            slots = pl.ds(u * SUB, SUB)
            self.ring_copy(t, u).wait_recv()
            self.ring[t, slots] += self.half[self.piece(t + 1), slots]
            if t + 1 < RING - 1:
                self.ring_copy(t + 1, u).start()

    def spread(self, start):
        held, me = self.ring.at[RING - 2], self.low * RING + self.chip

        def each(j, carry):
            chip, low = lax.rem(j, RING), lax.div(j, RING)
            self.plane_copy(held.at[chip], self.plane.at[0, me], 0, 2 * chip + self.core, low, start)
            return carry

        lax.fori_loop(0, 2 * RING, each, 0)
        for low in range(2):
            self.plane_copy(held.at[RING], self.plane.at[1, me], 1, 2 * self.z + self.core, low, start)

    def plane_copy(self, src, dst, k, s, low, start):
        is_self = (s == self.s) & (low == self.low)

        @pl.when(jnp.logical_not(is_self))
        def _():
            copy = pltpu.make_async_remote_copy(
                src_ref=src,
                dst_ref=dst,
                send_sem=self.plane_sems.at[0, k],
                recv_sem=self.plane_sems.at[1, k],
                device_id=(s, low * RING + self.z),
                device_id_type=MESH,
            )
            if start:
                copy.start()
            else:
                copy.wait_send()

        if start:

            @pl.when(is_self)
            def _():
                self.plane[k, self.low * RING + self.chip] = self.ring[
                    RING - 2, self.chip if k == 0 else RING
                ]

    def z_copy(self, k, j):
        rows = pl.ds(pl.multiple_of(self.z * 8, 8) if k == 0 else RING * 8, 8)
        return pltpu.make_async_remote_copy(
            src_ref=self.last.at[k],
            dst_ref=self.out.at[rows],
            send_sem=self.z_sems.at[0, k],
            recv_sem=self.z_sems.at[1, k],
            device_id=(self.s, self.low * RING + lax.rem(self.z + j, RING)),
            device_id_type=MESH,
        )

    def to_all_z(self, k, start):
        def each(j, carry):
            copy = self.z_copy(k, j)
            if start:
                copy.start()
            else:
                copy.wait_send()
            return carry

        lax.fori_loop(1, RING, each, 0)

    def gather(self):
        for k in range(2):

            @pl.when((self.chip == self.z) | (k == 0))
            def _():
                whole = self.plane.at[k, pl.ds(0, 2 * RING - 1)]
                pltpu.make_async_copy(whole, whole, self.plane_sems.at[1, k]).wait()
                total = self.plane[k, 0]
                for i in range(1, 2 * RING):
                    total = total + self.plane[k, i]
                self.last[k] = total
                self.to_all_z(k, True)
                rows = pl.ds(pl.multiple_of(self.z * 8, 8) if k == 0 else RING * 8, 8)
                self.out[rows] = total

    def finish(self):
        whole = self.plane.at[0, pl.ds(0, RING - 1)]
        pltpu.make_async_copy(whole, whole, self.z_sems.at[1, 0]).wait()
        self.to_all_z(0, False)

        @pl.when(self.chip == self.z)
        def _():
            self.to_all_z(1, False)

        @pl.when(self.chip != self.z)
        def _():
            one = self.plane.at[1, 0]
            pltpu.make_async_copy(one, one, self.z_sems.at[1, 1]).wait()

        self.spread(False)
        for t in range(RING - 1):
            for u in range(SLABS // SUB):
                self.ring_copy(t, u).wait_send()


def columns_of(width):
    step = 384 if width % 384 == 0 else width
    return [pl.ds(i, step) for i in range(0, width, step)]


def dot(a, b, over):
    return lax.dot_general(a, b, ((over[:1], over[1:]), ((), ())), preferred_element_type=jnp.float32)


class Attention:
    def __init__(self, part, frames, places, weight, arrived, results, scratch):
        self.part, self.frames, self.places, self.weight = part, frames, places, weight
        self.query, self.key, self.value, self.grad = arrived
        self.projected, self.grad_query, self.grad_key, self.grad_value = results
        self.cot, self.attn, self.bias, self.probs = scratch
        self.width = weight.shape[0]
        self.head_dim = self.width // HEADS
        self.count = self.bias.shape[0]

    def rows(self, c):
        return pl.ds(c * self.count, self.count)

    def live(self, c):
        row = lax.broadcasted_iota(jnp.int32, (self.count, 1), 0)
        place = lax.axis_index("seq") * self.part + row % self.part
        return (row // self.part < self.frames[c]) & (place < self.places[c])

    def window(self, h):
        low = jnp.minimum((h * self.head_dim) // 128 * 128, self.width - 256)
        lane = lax.broadcasted_iota(jnp.int32, (self.count, 256), 1) + low
        inside = (lane >= h * self.head_dim) & (lane < (h + 1) * self.head_dim)
        return pl.ds(pl.multiple_of(low, 128), 256), inside

    def forward(self, c):
        rows, count, part = self.rows(c), self.count, self.part
        key_row = lax.broadcasted_iota(jnp.int32, (count, count), 0)
        query_row = lax.broadcasted_iota(jnp.int32, (count, count), 1)
        allowed = (key_row % part == query_row % part) & (key_row // part < self.frames[c])
        self.bias[...] = jnp.where(allowed, 0.0, -1e30)
        live = self.live(c)
        scale = math.log2(math.e) / math.sqrt(self.head_dim)

        def head(h, carry):
            window, inside = self.window(h)
            query = jnp.where(inside, self.query[rows, window], 0.0).astype(jnp.bfloat16)
            scores = dot(self.key[rows, window], query, (1, 1)) + self.bias[...]
            highest = jnp.max(scores, axis=0, keepdims=True)
            expo = jnp.exp2((scores - highest) * scale)
            weights = expo * (1.0 / jnp.sum(expo, axis=0, keepdims=True))
            self.probs[h] = weights
            mixed = dot(weights.astype(jnp.bfloat16), self.value[rows, window], (0, 0))
            mixed = jnp.where(live, mixed, 0.0).astype(jnp.bfloat16)
            self.attn[rows, window] = jnp.where(inside, mixed, self.attn[rows, window])
            return carry

        lax.fori_loop(0, HEADS, head, 0)

    def cotangent(self, c):
        live = self.live(c)
        for cols in columns_of(self.width):
            wide = dot(self.grad[self.rows(c), :], self.weight[:, cols], (1, 0))
            self.cot[:, cols] = jnp.where(live, wide, 0.0).astype(jnp.bfloat16)

    def project(self, c):
        for cols in columns_of(self.width):
            wide = dot(self.attn[self.rows(c), :], self.weight[cols, :], (1, 1))
            self.projected[self.rows(c), cols] = wide.astype(jnp.bfloat16)

    def backward(self, c, first, past):
        rows = self.rows(c)
        inv_root = 1.0 / math.sqrt(self.head_dim)

        def head(h, carry):
            window, inside = self.window(h)
            key = self.key[rows, window]
            query = jnp.where(inside, self.query[rows, window], 0.0).astype(jnp.bfloat16)
            cot = jnp.where(inside, self.cot[:, window], 0.0).astype(jnp.bfloat16)
            weights = self.probs[h]

            def keep(target, found):
                found = found.astype(jnp.bfloat16)
                target[rows, window] = jnp.where(inside, found, target[rows, window])

            keep(self.grad_value, dot(weights.astype(jnp.bfloat16), cot, (1, 0)))
            grad_attn = dot(self.value[rows, window], cot, (1, 1))
            delta = jnp.sum(weights * grad_attn, axis=0, keepdims=True)
            grad_score = weights * (grad_attn - delta) * inv_root
            coarse = grad_score.astype(jnp.bfloat16)
            fine = (grad_score - coarse.astype(jnp.float32)).astype(jnp.bfloat16)
            keep(self.grad_query, dot(coarse, key, (0, 0)) + dot(fine, key, (0, 0)))
            keep(self.grad_key, dot(coarse, query, (1, 0)) + dot(fine, query, (1, 0)))
            return carry

        lax.fori_loop(first, past, head, 0)

    def weight_term(self, term):
        for cols in columns_of(self.width):
            found = dot(self.grad[:, cols], self.attn[...], (0, 0))
            for k in range(cols.size // 8):
                term[slab_place(cols.start // 8 + k)] = found[8 * k : 8 * k + 8]


class Exchange:
    def __init__(self, n, clips, part, sems):
        self.n, self.clips, self.part = n, clips, part
        self.send, self.recv, self.local = sems
        self.me, self.rep = lax.axis_index("seq"), lax.axis_index("rep")

    def start(self, c, a, here, place):
        pltpu.make_async_copy(here(self.me), place, self.local.at[c, a]).start()

        def push(j, carry):
            peer = lax.rem(self.me + j, self.n)
            pltpu.make_async_remote_copy(
                src_ref=here(peer),
                dst_ref=place,
                send_sem=self.send.at[c, a],
                recv_sem=self.recv.at[c, a],
                device_id=(peer, self.rep),
                device_id_type=MESH,
            ).start()
            return carry

        lax.fori_loop(1, self.n, push, 0)

    def tile(self, array, c, owner):
        return array.at[pl.ds(pl.multiple_of((c * self.n + owner) * self.part, self.part), self.part)]

    def strip(self, array, c, owner):
        return array.at[c, 0, pl.ds(pl.multiple_of(owner * self.part, self.part), self.part)]

    def bring(self, c, a, source, target):
        self.start(c, a, lambda peer: self.strip(source, c, peer), self.tile(target, c, self.me))

    def give(self, c, a, source, target):
        self.start(c, a, lambda peer: self.tile(source, c, peer), self.strip(target, c, self.me))

    def wait(self, sem, count, array):
        some = array.at[pl.ds(0, count * self.part)]
        pltpu.make_async_copy(some, some, sem).wait()

    def arrived(self, c, a, array):
        self.wait(self.local.at[c, a], 1, array)
        self.wait(self.recv.at[c, a], self.n - 1, array)

    def left(self, c, a, array):
        self.wait(self.send.at[c, a], self.n - 1, array)


def fused_kernel(n, part, frames, places, *refs):
    sources, weight, targets, out = refs[:4], refs[4], refs[5:9], refs[9]
    arrived, results, scratch = refs[10:14], refs[14:18], refs[18:22]
    term, half, ring, plane, last = refs[22:27]
    clips = sources[0].shape[0]
    inward, outward = Exchange(n, clips, part, refs[27:30]), Exchange(n, clips, part, refs[30:33])
    weight_sum = WeightSum(term, out, half, ring, plane, last, refs[33:])
    work = Attention(part, frames, places, weight, arrived, results, scratch)
    greet([row_peers(n)] + weight_sum.peers())
    for c in range(clips):
        for a in range(4):
            inward.bring(c, a, sources[a], arrived[a])

    def give(c, a):
        outward.give(c, a, results[a], targets[a])

    end = clips - 1
    for c in range(clips):
        for a in range(3):
            inward.arrived(c, a, arrived[a])
        work.forward(c)
        inward.arrived(c, 3, arrived[3])
        if c < end:
            work.cotangent(c)
            work.backward(c, 0, HEADS)
            work.project(c)
    work.weight_term(term)
    weight_sum.half_copy().start()
    for c in range(end):
        for a in range(4):
            give(c, a)
    work.project(end)
    give(end, 0)
    work.cotangent(end)
    weight_sum.add_half()
    weight_sum.ring_start()
    for t in range(RING - 1):
        if t * TOGETHER < HEADS:
            work.backward(end, t * TOGETHER, (t + 1) * TOGETHER)
            if (t + 1) * TOGETHER == HEADS:
                for a in range(1, 4):
                    give(end, a)
        weight_sum.ring_step(t)
    weight_sum.spread(True)
    weight_sum.gather()
    weight_sum.finish()
    for c in range(clips):
        for a in range(4):
            inward.left(c, a, arrived[a])
            outward.arrived(c, a, results[a])
            outward.left(c, a, results[a])


def fused(n, arrays, weight, frames, places):
    clips, _, all_places, width = arrays[0].shape
    part = all_places // n
    rows = n * part
    dma = pltpu.SemaphoreType.DMA
    smem, vmem, anywhere = (
        pl.BlockSpec(memory_space=space) for space in (pltpu.SMEM, pltpu.VMEM, pl.ANY)
    )
    return pl.pallas_call(
        functools.partial(fused_kernel, n, part),
        out_shape=[jax.ShapeDtypeStruct(arrays[0].shape, jnp.bfloat16)] * 4
        + [jax.ShapeDtypeStruct((SLABS * 8, width), jnp.float32)],
        in_specs=[smem, smem] + [anywhere] * 4 + [vmem],
        out_specs=[anywhere] * 4 + [vmem],
        scratch_shapes=[pltpu.VMEM((clips * rows, width), jnp.bfloat16)] * 8
        + [
            pltpu.VMEM((rows, width), jnp.bfloat16),
            pltpu.VMEM((clips * rows, width), jnp.bfloat16),
            pltpu.VMEM((rows, rows), jnp.float32),
            pltpu.VMEM((HEADS, rows, rows), jnp.float32),
            pltpu.VMEM((2, RING, SLABS, 8, width), jnp.float32),
            pltpu.VMEM((RING, SLABS, 8, width), jnp.float32),
            pltpu.VMEM((RING - 1, SLABS, 8, width), jnp.float32),
            pltpu.VMEM((2, 2 * RING, 8, width), jnp.float32),
            pltpu.VMEM((2, 8, width), jnp.float32),
        ]
        + [dma((clips, 4))] * 6
        + [dma((2,)), dma((RING - 1, SLABS // SUB)), dma((RING - 1, SLABS // SUB)), dma((2, 2)), dma((2, 2))],
        compiler_params=pltpu.CompilerParams(
            collective_id=0, has_side_effects=True, vmem_limit_bytes=VMEM_BYTES
        ),
    )(frames, places, *arrays, weight)


def deliver_kernel(*refs):
    count = (len(refs) - 2) // 3
    sources, targets, held = refs[:count], refs[count : 2 * count], refs[2 * count : 3 * count]
    fetch = [pltpu.make_async_copy(sources[i], held[i], refs[-2].at[i]) for i in range(count)]
    store = [pltpu.make_async_copy(held[i], targets[i], refs[-1].at[i]) for i in range(count)]
    for copy in fetch:
        copy.start()
    for i in range(count):
        fetch[i].wait()
        store[i].start()
    for copy in store:
        copy.wait()


def deliver(arrays):
    count = len(arrays)
    return pl.pallas_call(
        deliver_kernel,
        out_shape=[jax.ShapeDtypeStruct(a.shape, a.dtype) for a in arrays],
        in_specs=[pl.BlockSpec(memory_space=pl.ANY)] * count,
        out_specs=[pl.BlockSpec(memory_space=pl.ANY)] * count,
        scratch_shapes=[pltpu.VMEM(a.shape, a.dtype) for a in arrays]
        + [pltpu.SemaphoreType.DMA((count,))] * 2,
        compiler_params=pltpu.CompilerParams(vmem_limit_bytes=VMEM_BYTES),
    )(*arrays)


def shards(query_rows, key_rows, value_rows, out_grad, out_weight, frame_count, pos_count):
    n = lax.axis_size("seq")
    arrays = (query_rows, key_rows, value_rows, out_grad)
    return tuple(deliver(fused(n, arrays, out_weight, frame_count, pos_count)))


def solution(mesh):
    rows = P("rep", "seq", None, None)
    return jax.shard_map(
        shards,
        mesh=mesh,
        in_specs=(rows, rows, rows, rows, P(), P("rep"), P("rep")),
        out_specs=(rows, rows, rows, rows, P("seq", None)),
        check_vma=False,
    )
```

```python
import functools
import math

import jax
import jax.numpy as jnp
from jax import lax
from jax.experimental import pallas as pl
from jax.experimental.pallas import tpu as pltpu
from jax.sharding import PartitionSpec as P

HEADS = 16
RING = 8
SLABS = 9
TOGETHER = 2
BATCH = 3
HALVES = (pl.ds(0, 640), pl.ds(640, 512))
SUB = 3
MESH = pl.DeviceIdType.MESH
VMEM_BYTES = 56 << 20


def greet(peers):
    barrier = pltpu.get_barrier_semaphore()
    for first, count, peer_of in peers:

        def signal(j, carry):
            pl.semaphore_signal(barrier, inc=1, device_id=peer_of(j), device_id_type=MESH)
            return carry

        lax.fori_loop(first, first + count, signal, 0)
    pl.semaphore_wait(barrier, sum(count for _, count, _ in peers))


def row_peers(n):
    s, r = lax.axis_index("seq"), lax.axis_index("rep")
    return (1, n - 1, lambda j: (lax.rem(s + j, n), r))


def slab_place(slab):
    block, i = slab // SLABS, slab % SLABS
    core, chip = block % 2, block // 2
    return (core, i, chip) if i < RING else (core, chip, RING)


class WeightSum:
    def __init__(self, term, out, half, ring, plane, last, sems):
        self.term, self.out, self.half, self.ring, self.plane, self.last = (
            term, out, half, ring, plane, last,
        )
        (self.half_sems, self.ring_send, self.ring_recv, self.plane_sems, self.z_sems) = sems
        self.s, self.r = lax.axis_index("seq"), lax.axis_index("rep")
        self.core, self.chip = lax.rem(self.s, 2), lax.div(self.s, 2)
        self.z, self.low = lax.rem(self.r, RING), lax.div(self.r, RING)

    def peers(self):
        s, r, core, z, low = self.s, self.r, self.core, self.z, self.low
        other = (1 - low) * RING
        return [
            (0, RING, lambda j: (2 * j + core, other + z)),
            (1, RING - 1, lambda j: (s, low * RING + lax.rem(z + j, RING))),
            (1, RING - 1, lambda j: (s, other + lax.rem(z + j, RING))),
        ]

    def half_copy(self):
        return pltpu.make_async_remote_copy(
            src_ref=self.term.at[1 - self.core],
            dst_ref=self.half,
            send_sem=self.half_sems.at[0],
            recv_sem=self.half_sems.at[1],
            device_id=(self.s + 1 - 2 * self.core, self.r),
            device_id_type=MESH,
        )

    def add_half(self):
        self.half_copy().wait()

        def add(j, carry):
            self.half[j] += self.term[self.core, j]
            return carry

        lax.fori_loop(0, RING, add, 0)

    def piece(self, t):
        way = 1 - 2 * self.core
        return lax.rem(self.z - way * (t + 1) + 2 * RING, RING)

    def ring_copy(self, t, u):
        way = 1 - 2 * self.core
        slots = pl.ds(u * SUB, SUB)
        return pltpu.make_async_remote_copy(
            src_ref=self.half.at[self.piece(0), slots] if t == 0 else self.ring.at[t - 1, slots],
            dst_ref=self.ring.at[t, slots],
            send_sem=self.ring_send.at[t, u],
            recv_sem=self.ring_recv.at[t, u],
            device_id=(self.s, self.low * RING + lax.rem(self.z + way + RING, RING)),
            device_id_type=MESH,
        )

    def ring_start(self):
        for u in range(SLABS // SUB):
            self.ring_copy(0, u).start()

    def ring_step(self, t, u):
        slots = pl.ds(u * SUB, SUB)
        self.ring_copy(t, u).wait_recv()
        self.ring[t, slots] += self.half[self.piece(t + 1), slots]
        if t + 1 < RING - 1:
            self.ring_copy(t + 1, u).start()

    def spread(self, start):
        me = self.low * RING + self.chip
        for low in range(2):

            def each(chip, carry):
                self.plane_copy(chip, 0, me, 2 * chip + self.core, low, start)
                return carry

            lax.fori_loop(0, RING, each, 0)
            self.plane_copy(RING, 1, me, 2 * self.z + self.core, low, start)

    def plane_copy(self, slot, k, me, s, low, start):
        is_self = (s == self.s) & (low == self.low)
        cols = HALVES[low]
        held = self.ring.at[RING - 2, slot, :, cols]

        @pl.when(jnp.logical_not(is_self))
        def _():
            copy = pltpu.make_async_remote_copy(
                src_ref=held,
                dst_ref=self.plane.at[k, me, :, pl.ds(0, cols.size)],
                send_sem=self.plane_sems.at[0, k],
                recv_sem=self.plane_sems.at[1, k],
                device_id=(s, low * RING + self.z),
                device_id_type=MESH,
            )
            if start:
                copy.start()
            else:
                copy.wait_send()

        if start:

            @pl.when(is_self)
            def _():
                self.plane[k, me, :, pl.ds(0, cols.size)] = self.ring[RING - 2, slot, :, cols]

    def own_rows(self, k):
        return pl.ds(pl.multiple_of(self.z * 8, 8) if k == 0 else RING * 8, 8)

    def to_all(self, k, low, start):
        cols = HALVES[low]

        def each(j, carry):
            copy = pltpu.make_async_remote_copy(
                src_ref=self.last.at[k, :, pl.ds(0, cols.size)],
                dst_ref=self.out.at[self.own_rows(k), cols],
                send_sem=self.z_sems.at[0, k],
                recv_sem=self.z_sems.at[1 + low, k],
                device_id=(self.s, lax.rem(self.r + j, 2 * RING)),
                device_id_type=MESH,
            )
            if start:
                copy.start()
            else:
                copy.wait_send()
            return carry

        lax.fori_loop(1, 2 * RING, each, 0)

    def gather(self):
        for k in range(2):
            for low in range(2):

                @pl.when((self.low == low) & ((self.chip == self.z) | (k == 0)))
                def _():
                    cols = HALVES[low]
                    some = pl.ds(0, cols.size)
                    whole = self.plane.at[k, pl.ds(0, 2 * RING - 1), :, some]
                    pltpu.make_async_copy(whole, whole, self.plane_sems.at[1, k]).wait()
                    total = self.plane[k, 0, :, some]
                    for i in range(1, 2 * RING):
                        total = total + self.plane[k, i, :, some]
                    self.last[k, :, some] = total
                    self.to_all(k, low, True)
                    self.out[self.own_rows(k), cols] = total

    def finish(self):
        for low in range(2):
            mine = self.low == low
            some = pl.ds(0, HALVES[low].size)
            for count, is_count in ((RING - 1, mine), (RING, jnp.logical_not(mine))):

                @pl.when(is_count)
                def _():
                    whole = self.plane.at[0, pl.ds(0, count), :, some]
                    pltpu.make_async_copy(whole, whole, self.z_sems.at[1 + low, 0]).wait()

            @pl.when(jnp.logical_not(mine & (self.chip == self.z)))
            def _():
                one = self.plane.at[1, 0, :, some]
                pltpu.make_async_copy(one, one, self.z_sems.at[1 + low, 1]).wait()

            for k in range(2):

                @pl.when(mine & ((self.chip == self.z) | (k == 0)))
                def _():
                    self.to_all(k, low, False)

        self.spread(False)
        for t in range(RING - 1):
            for u in range(SLABS // SUB):
                self.ring_copy(t, u).wait_send()


def columns_of(width):
    step = 384 if width % 384 == 0 else width
    return [pl.ds(i, step) for i in range(0, width, step)]


def dot(a, b, over):
    return lax.dot_general(a, b, ((over[:1], over[1:]), ((), ())), preferred_element_type=jnp.float32)


class Attention:
    def __init__(self, part, frames, places, weight, arrived, results, scratch):
        self.part, self.frames, self.places, self.weight = part, frames, places, weight
        self.query, self.key, self.value, self.grad = arrived
        self.projected, self.grad_query, self.grad_key, self.grad_value = results
        self.cot, self.attn, self.bias, self.probs = scratch
        self.width = weight.shape[0]
        self.head_dim = self.width // HEADS
        self.count = self.bias.shape[0]

    def rows(self, c):
        return pl.ds(c * self.count, self.count)

    def live(self, c):
        row = lax.broadcasted_iota(jnp.int32, (self.count, 1), 0)
        place = lax.axis_index("seq") * self.part + row % self.part
        return (row // self.part < self.frames[c]) & (place < self.places[c])

    def window(self, h):
        low = jnp.minimum((h * self.head_dim) // 128 * 128, self.width - 256)
        lane = lax.broadcasted_iota(jnp.int32, (self.count, 256), 1) + low
        inside = (lane >= h * self.head_dim) & (lane < (h + 1) * self.head_dim)
        return pl.ds(pl.multiple_of(low, 128), 256), inside

    def forward(self, c):
        rows, count, part = self.rows(c), self.count, self.part
        key_row = lax.broadcasted_iota(jnp.int32, (count, count), 0)
        query_row = lax.broadcasted_iota(jnp.int32, (count, count), 1)
        allowed = (key_row % part == query_row % part) & (key_row // part < self.frames[c])
        self.bias[...] = jnp.where(allowed, 0.0, -1e30)
        live = self.live(c)
        scale = math.log2(math.e) / math.sqrt(self.head_dim)

        def head(h, carry):
            window, inside = self.window(h)
            query = jnp.where(inside, self.query[rows, window], 0.0).astype(jnp.bfloat16)
            scores = dot(self.key[rows, window], query, (1, 1)) + self.bias[...]
            highest = jnp.max(scores, axis=0, keepdims=True)
            expo = jnp.exp2((scores - highest) * scale)
            weights = expo * (1.0 / jnp.sum(expo, axis=0, keepdims=True))
            self.probs[h] = weights
            mixed = dot(weights.astype(jnp.bfloat16), self.value[rows, window], (0, 0))
            mixed = jnp.where(live, mixed, 0.0).astype(jnp.bfloat16)
            self.attn[rows, window] = jnp.where(inside, mixed, self.attn[rows, window])
            return carry

        lax.fori_loop(0, HEADS, head, 0)

    def cotangent(self, c):
        live = self.live(c)
        for cols in columns_of(self.width):
            wide = dot(self.grad[self.rows(c), :], self.weight[:, cols], (1, 0))
            self.cot[:, cols] = jnp.where(live, wide, 0.0).astype(jnp.bfloat16)

    def project(self, c):
        for cols in columns_of(self.width):
            wide = dot(self.attn[self.rows(c), :], self.weight[cols, :], (1, 1))
            self.projected[self.rows(c), cols] = wide.astype(jnp.bfloat16)

    def backward(self, c, first, past):
        rows = self.rows(c)
        inv_root = 1.0 / math.sqrt(self.head_dim)

        def head(h, carry):
            window, inside = self.window(h)
            key = self.key[rows, window]
            query = jnp.where(inside, self.query[rows, window], 0.0).astype(jnp.bfloat16)
            cot = jnp.where(inside, self.cot[:, window], 0.0).astype(jnp.bfloat16)
            weights = self.probs[h]

            def keep(target, found):
                found = found.astype(jnp.bfloat16)
                target[rows, window] = jnp.where(inside, found, target[rows, window])

            keep(self.grad_value, dot(weights.astype(jnp.bfloat16), cot, (1, 0)))
            grad_attn = dot(self.value[rows, window], cot, (1, 1))
            delta = jnp.sum(weights * grad_attn, axis=0, keepdims=True)
            grad_score = weights * (grad_attn - delta) * inv_root
            coarse = grad_score.astype(jnp.bfloat16)
            fine = (grad_score - coarse.astype(jnp.float32)).astype(jnp.bfloat16)
            keep(self.grad_query, dot(coarse, key, (0, 0)) + dot(fine, key, (0, 0)))
            keep(self.grad_key, dot(coarse, query, (1, 0)) + dot(fine, query, (1, 0)))
            return carry

        lax.fori_loop(first, past, head, 0)

    def weight_term(self, term):
        for cols in columns_of(self.width):
            found = dot(self.grad[:, cols], self.attn[...], (0, 0))
            for k in range(cols.size // 8):
                term[slab_place(cols.start // 8 + k)] = found[8 * k : 8 * k + 8]


class Exchange:
    def __init__(self, n, clips, part, sems):
        self.n, self.clips, self.part = n, clips, part
        self.send, self.recv, self.local = sems
        self.me, self.rep = lax.axis_index("seq"), lax.axis_index("rep")

    def start(self, c, a, here, place, first, past):
        if first == 0:
            pltpu.make_async_copy(here(self.me), place, self.local.at[c, a]).start()

        def push(j, carry):
            peer = lax.rem(self.me + j, self.n)
            pltpu.make_async_remote_copy(
                src_ref=here(peer),
                dst_ref=place,
                send_sem=self.send.at[c, a],
                recv_sem=self.recv.at[c, a],
                device_id=(peer, self.rep),
                device_id_type=MESH,
            ).start()
            return carry

        lax.fori_loop(max(first, 1), past, push, 0)

    def tile(self, array, c, owner):
        return array.at[pl.ds(pl.multiple_of((c * self.n + owner) * self.part, self.part), self.part)]

    def strip(self, array, c, owner):
        return array.at[c, 0, pl.ds(pl.multiple_of(owner * self.part, self.part), self.part)]

    def bring(self, c, a, source, target):
        self.start(c, a, lambda peer: self.strip(source, c, peer), self.tile(target, c, self.me), 0, self.n)

    def give(self, c, a, source, target, first, past):
        place = self.strip(target, c, self.me)
        self.start(c, a, lambda peer: self.tile(source, c, peer), place, first, past)

    def wait(self, sem, count, array):
        some = array.at[pl.ds(0, count * self.part)]
        pltpu.make_async_copy(some, some, sem).wait()

    def arrived(self, c, a, array):
        self.wait(self.local.at[c, a], 1, array)
        self.wait(self.recv.at[c, a], self.n - 1, array)

    def left(self, c, a, array):
        self.wait(self.send.at[c, a], self.n - 1, array)


def fused_kernel(n, part, frames, places, *refs):
    sources, weight_hbm, targets, out = refs[:4], refs[4], refs[5:9], refs[9]
    arrived, results, scratch = refs[10:14], refs[14:18], refs[18:22]
    term, half, ring, plane, last, weight, weight_sem = refs[22:29]
    clips = sources[0].shape[0]
    inward, outward = Exchange(n, clips, part, refs[29:32]), Exchange(n, clips, part, refs[32:35])
    weight_sum = WeightSum(term, out, half, ring, plane, last, refs[35:])
    work = Attention(part, frames, places, weight, arrived, results, scratch)
    fetch = pltpu.make_async_copy(weight_hbm, weight, weight_sem)
    fetch.start()
    greet([row_peers(n)] + weight_sum.peers())
    for c in range(clips):
        for a in range(4):
            inward.bring(c, a, sources[a], arrived[a])

    ready = []

    def offer(c, arrays):
        ready.extend((c, a, first) for a in arrays for first in range(0, n, BATCH))

    def give(batches):
        for c, a, first in ready[:batches]:
            outward.give(c, a, results[a], targets[a], first, min(first + BATCH, n))
        del ready[:batches]

    end = clips - 1
    for c in range(clips):
        for a in range(3):
            inward.arrived(c, a, arrived[a])
        if c == end:
            give(4)
        work.forward(c)
        inward.arrived(c, 3, arrived[3])
        if c == 0:
            fetch.wait()
        if c < end:
            work.cotangent(c)
            work.backward(c, 0, HEADS)
            work.project(c)
            offer(c, range(4))
    give(8)
    work.weight_term(term)
    weight_sum.half_copy().start()
    give(6)
    work.project(end)
    offer(end, [0])
    work.cotangent(end)
    weight_sum.add_half()
    weight_sum.ring_start()
    done = 0
    for t in range(RING - 1):
        for u in range(SLABS // SUB):
            if done < HEADS:
                work.backward(end, done, done + TOGETHER)
                done += TOGETHER
                if done == HEADS:
                    offer(end, range(1, 4))
            weight_sum.ring_step(t, u)
            give(1)
    weight_sum.spread(True)
    give(3)
    weight_sum.gather()
    give(len(ready))
    weight_sum.finish()
    for c in range(clips):
        for a in range(4):
            inward.left(c, a, arrived[a])
            outward.arrived(c, a, results[a])
            outward.left(c, a, results[a])


def fused(n, arrays, weight, frames, places):
    clips, _, all_places, width = arrays[0].shape
    part = all_places // n
    rows = n * part
    dma = pltpu.SemaphoreType.DMA
    smem, vmem, anywhere = (
        pl.BlockSpec(memory_space=space) for space in (pltpu.SMEM, pltpu.VMEM, pl.ANY)
    )
    return pl.pallas_call(
        functools.partial(fused_kernel, n, part),
        out_shape=[jax.ShapeDtypeStruct(arrays[0].shape, jnp.bfloat16)] * 4
        + [jax.ShapeDtypeStruct((SLABS * 8, width), jnp.float32)],
        in_specs=[smem, smem] + [anywhere] * 5,
        out_specs=[anywhere] * 4 + [vmem],
        scratch_shapes=[pltpu.VMEM((clips * rows, width), jnp.bfloat16)] * 8
        + [
            pltpu.VMEM((rows, width), jnp.bfloat16),
            pltpu.VMEM((clips * rows, width), jnp.bfloat16),
            pltpu.VMEM((rows, rows), jnp.float32),
            pltpu.VMEM((HEADS, rows, rows), jnp.float32),
            pltpu.VMEM((2, RING, SLABS, 8, width), jnp.float32),
            pltpu.VMEM((RING, SLABS, 8, width), jnp.float32),
            pltpu.VMEM((RING - 1, SLABS, 8, width), jnp.float32),
            pltpu.VMEM((2, 2 * RING, 8, 640), jnp.float32),
            pltpu.VMEM((2, 8, 640), jnp.float32),
            pltpu.VMEM((width, width), jnp.bfloat16),
            dma(()),
        ]
        + [dma((clips, 4))] * 6
        + [dma((2,)), dma((RING - 1, SLABS // SUB)), dma((RING - 1, SLABS // SUB)), dma((2, 2)), dma((3, 2))],
        compiler_params=pltpu.CompilerParams(
            collective_id=0, has_side_effects=True, vmem_limit_bytes=VMEM_BYTES
        ),
    )(frames, places, *arrays, weight)


def deliver_kernel(*refs):
    count = (len(refs) - 2) // 3
    sources, targets, held = refs[:count], refs[count : 2 * count], refs[2 * count : 3 * count]
    fetch = [pltpu.make_async_copy(sources[i], held[i], refs[-2].at[i]) for i in range(count)]
    store = [pltpu.make_async_copy(held[i], targets[i], refs[-1].at[i]) for i in range(count)]
    for copy in fetch:
        copy.start()
    for i in range(count):
        fetch[i].wait()
        store[i].start()
    for copy in store:
        copy.wait()


def deliver(arrays):
    count = len(arrays)
    return pl.pallas_call(
        deliver_kernel,
        out_shape=[jax.ShapeDtypeStruct(a.shape, a.dtype) for a in arrays],
        in_specs=[pl.BlockSpec(memory_space=pl.ANY)] * count,
        out_specs=[pl.BlockSpec(memory_space=pl.ANY)] * count,
        scratch_shapes=[pltpu.VMEM(a.shape, a.dtype) for a in arrays]
        + [pltpu.SemaphoreType.DMA((count,))] * 2,
        compiler_params=pltpu.CompilerParams(vmem_limit_bytes=VMEM_BYTES),
    )(*arrays)


def shards(query_rows, key_rows, value_rows, out_grad, out_weight, frame_count, pos_count):
    n = lax.axis_size("seq")
    arrays = (query_rows, key_rows, value_rows, out_grad)
    return tuple(deliver(fused(n, arrays, out_weight, frame_count, pos_count)))


def solution(mesh):
    rows = P("rep", "seq", None, None)
    return jax.shard_map(
        shards,
        mesh=mesh,
        in_specs=(rows, rows, rows, rows, P(), P("rep"), P("rep")),
        out_specs=(rows, rows, rows, rows, P("seq", None)),
        check_vma=False,
    )
```

```python
import functools
import math

import jax
import jax.numpy as jnp
from jax import lax
from jax.experimental import pallas as pl
from jax.experimental.pallas import tpu as pltpu
from jax.sharding import PartitionSpec as P

HEADS = 16
RING = 8
SLABS = 9
TOGETHER = 2
BATCH = 3
HALVES = (pl.ds(0, 640), pl.ds(640, 512))
SUB = 3
MESH = pl.DeviceIdType.MESH
VMEM_BYTES = 56 << 20


def greet(peers):
    barrier = pltpu.get_barrier_semaphore()
    for first, count, peer_of in peers:

        def signal(j, carry):
            pl.semaphore_signal(barrier, inc=1, device_id=peer_of(j), device_id_type=MESH)
            return carry

        lax.fori_loop(first, first + count, signal, 0)
    pl.semaphore_wait(barrier, sum(count for _, count, _ in peers))


def row_peers(n):
    s, r = lax.axis_index("seq"), lax.axis_index("rep")
    return (1, n - 1, lambda j: (lax.rem(s + j, n), r))


def slab_place(slab):
    block, i = slab // SLABS, slab % SLABS
    core, chip = block % 2, block // 2
    return (core, i, chip) if i < RING else (core, chip, RING)


class WeightSum:
    def __init__(self, term, out, half, ring, plane, last, sems):
        self.term, self.out, self.half, self.ring, self.plane, self.last = (
            term, out, half, ring, plane, last,
        )
        (self.half_sems, self.ring_send, self.ring_recv, self.plane_sems, self.z_sems) = sems
        self.s, self.r = lax.axis_index("seq"), lax.axis_index("rep")
        self.core, self.chip = lax.rem(self.s, 2), lax.div(self.s, 2)
        self.z, self.low = lax.rem(self.r, RING), lax.div(self.r, RING)

    def peers(self):
        s, r, core, z, low = self.s, self.r, self.core, self.z, self.low
        other = (1 - low) * RING
        return [
            (0, RING, lambda j: (2 * j + core, other + z)),
            (1, RING - 1, lambda j: (s, low * RING + lax.rem(z + j, RING))),
            (1, RING - 1, lambda j: (s, other + lax.rem(z + j, RING))),
        ]

    def half_copy(self):
        return pltpu.make_async_remote_copy(
            src_ref=self.term.at[1 - self.core],
            dst_ref=self.half,
            send_sem=self.half_sems.at[0],
            recv_sem=self.half_sems.at[1],
            device_id=(self.s + 1 - 2 * self.core, self.r),
            device_id_type=MESH,
        )

    def send_half(self, first, past):
        for core in range(2):

            @pl.when(self.core == 1 - core)
            def _():
                for slab in range(first, past):
                    place = slab_place(slab)
                    if place[0] == core:
                        pltpu.make_async_remote_copy(
                            src_ref=self.term.at[place],
                            dst_ref=self.half.at[place[1:]],
                            send_sem=self.half_sems.at[0],
                            recv_sem=self.half_sems.at[1],
                            device_id=(self.s + 1 - 2 * self.core, self.r),
                            device_id_type=MESH,
                        ).start()

    def add_half(self):
        self.half_copy().wait()

        def add(j, carry):
            self.half[j] += self.term[self.core, j]
            return carry

        lax.fori_loop(0, RING, add, 0)

    def piece(self, t):
        way = 1 - 2 * self.core
        return lax.rem(self.z - way * (t + 1) + 2 * RING, RING)

    def ring_copy(self, t, u):
        way = 1 - 2 * self.core
        slots = pl.ds(u * SUB, SUB)
        return pltpu.make_async_remote_copy(
            src_ref=self.half.at[self.piece(0), slots] if t == 0 else self.ring.at[t - 1, slots],
            dst_ref=self.ring.at[t, slots],
            send_sem=self.ring_send.at[t, u],
            recv_sem=self.ring_recv.at[t, u],
            device_id=(self.s, self.low * RING + lax.rem(self.z + way + RING, RING)),
            device_id_type=MESH,
        )

    def ring_start(self):
        for u in range(SLABS // SUB):
            self.ring_copy(0, u).start()

    def ring_step(self, t, u):
        slots = pl.ds(u * SUB, SUB)
        self.ring_copy(t, u).wait_recv()
        self.ring[t, slots] += self.half[self.piece(t + 1), slots]
        if t + 1 < RING - 1:
            self.ring_copy(t + 1, u).start()

    def spread(self, start):
        me = self.low * RING + self.chip
        for low in range(2):

            def each(chip, carry):
                self.plane_copy(chip, 0, me, 2 * chip + self.core, low, start)
                return carry

            lax.fori_loop(0, RING, each, 0)
            self.plane_copy(RING, 1, me, 2 * self.z + self.core, low, start)

    def plane_copy(self, slot, k, me, s, low, start):
        is_self = (s == self.s) & (low == self.low)
        cols = HALVES[low]
        held = self.ring.at[RING - 2, slot, :, cols]

        @pl.when(jnp.logical_not(is_self))
        def _():
            copy = pltpu.make_async_remote_copy(
                src_ref=held,
                dst_ref=self.plane.at[k, me, :, pl.ds(0, cols.size)],
                send_sem=self.plane_sems.at[0, k],
                recv_sem=self.plane_sems.at[1, k],
                device_id=(s, low * RING + self.z),
                device_id_type=MESH,
            )
            if start:
                copy.start()
            else:
                copy.wait_send()

        if start:

            @pl.when(is_self)
            def _():
                self.plane[k, me, :, pl.ds(0, cols.size)] = self.ring[RING - 2, slot, :, cols]

    def own_rows(self, k):
        return pl.ds(pl.multiple_of(self.z * 8, 8) if k == 0 else RING * 8, 8)

    def to_all(self, k, low, start):
        cols = HALVES[low]

        def each(j, carry):
            copy = pltpu.make_async_remote_copy(
                src_ref=self.last.at[k, :, pl.ds(0, cols.size)],
                dst_ref=self.out.at[self.own_rows(k), cols],
                send_sem=self.z_sems.at[0, k],
                recv_sem=self.z_sems.at[1 + low, k],
                device_id=(self.s, lax.rem(self.r + j, 2 * RING)),
                device_id_type=MESH,
            )
            if start:
                copy.start()
            else:
                copy.wait_send()
            return carry

        lax.fori_loop(1, 2 * RING, each, 0)

    def gather(self):
        for k in range(2):
            for low in range(2):

                @pl.when((self.low == low) & ((self.chip == self.z) | (k == 0)))
                def _():
                    cols = HALVES[low]
                    some = pl.ds(0, cols.size)
                    whole = self.plane.at[k, pl.ds(0, 2 * RING - 1), :, some]
                    pltpu.make_async_copy(whole, whole, self.plane_sems.at[1, k]).wait()
                    total = self.plane[k, 0, :, some]
                    for i in range(1, 2 * RING):
                        total = total + self.plane[k, i, :, some]
                    self.last[k, :, some] = total
                    self.to_all(k, low, True)
                    self.out[self.own_rows(k), cols] = total

    def finish(self):
        for low in range(2):
            mine = self.low == low
            some = pl.ds(0, HALVES[low].size)
            for count, is_count in ((RING - 1, mine), (RING, jnp.logical_not(mine))):

                @pl.when(is_count)
                def _():
                    whole = self.plane.at[0, pl.ds(0, count), :, some]
                    pltpu.make_async_copy(whole, whole, self.z_sems.at[1 + low, 0]).wait()

            @pl.when(jnp.logical_not(mine & (self.chip == self.z)))
            def _():
                one = self.plane.at[1, 0, :, some]
                pltpu.make_async_copy(one, one, self.z_sems.at[1 + low, 1]).wait()

            for k in range(2):

                @pl.when(mine & ((self.chip == self.z) | (k == 0)))
                def _():
                    self.to_all(k, low, False)

        self.spread(False)
        for t in range(RING - 1):
            for u in range(SLABS // SUB):
                self.ring_copy(t, u).wait_send()


def columns_of(width):
    step = 384 if width % 384 == 0 else width
    return [pl.ds(i, step) for i in range(0, width, step)]


def dot(a, b, over):
    return lax.dot_general(a, b, ((over[:1], over[1:]), ((), ())), preferred_element_type=jnp.float32)


class Attention:
    def __init__(self, part, frames, places, weight, arrived, results, scratch):
        self.part, self.frames, self.places, self.weight = part, frames, places, weight
        self.query, self.key, self.value, self.grad = arrived
        self.projected, self.grad_query, self.grad_key, self.grad_value = results
        self.cot, self.attn, self.bias, self.probs = scratch
        self.width = weight.shape[0]
        self.head_dim = self.width // HEADS
        self.count = self.bias.shape[0]

    def rows(self, c):
        return pl.ds(c * self.count, self.count)

    def live(self, c):
        row = lax.broadcasted_iota(jnp.int32, (self.count, 1), 0)
        place = lax.axis_index("seq") * self.part + row % self.part
        return (row // self.part < self.frames[c]) & (place < self.places[c])

    def window(self, h):
        low = jnp.minimum((h * self.head_dim) // 128 * 128, self.width - 256)
        lane = lax.broadcasted_iota(jnp.int32, (self.count, 256), 1) + low
        inside = (lane >= h * self.head_dim) & (lane < (h + 1) * self.head_dim)
        return pl.ds(pl.multiple_of(low, 128), 256), inside

    def forward(self, c):
        rows, count, part = self.rows(c), self.count, self.part
        key_row = lax.broadcasted_iota(jnp.int32, (count, count), 0)
        query_row = lax.broadcasted_iota(jnp.int32, (count, count), 1)
        allowed = (key_row % part == query_row % part) & (key_row // part < self.frames[c])
        self.bias[...] = jnp.where(allowed, 0.0, -1e30)
        live = self.live(c)
        scale = math.log2(math.e) / math.sqrt(self.head_dim)

        def head(h, carry):
            window, inside = self.window(h)
            query = jnp.where(inside, self.query[rows, window], 0.0).astype(jnp.bfloat16)
            scores = dot(self.key[rows, window], query, (1, 1)) + self.bias[...]
            highest = jnp.max(scores, axis=0, keepdims=True)
            expo = jnp.exp2((scores - highest) * scale)
            weights = expo * (1.0 / jnp.sum(expo, axis=0, keepdims=True))
            self.probs[h] = weights
            mixed = dot(weights.astype(jnp.bfloat16), self.value[rows, window], (0, 0))
            mixed = jnp.where(live, mixed, 0.0).astype(jnp.bfloat16)
            self.attn[rows, window] = jnp.where(inside, mixed, self.attn[rows, window])
            return carry

        lax.fori_loop(0, HEADS, head, 0)

    def cotangent(self, c):
        live = self.live(c)
        for cols in columns_of(self.width):
            wide = dot(self.grad[self.rows(c), :], self.weight[:, cols], (1, 0))
            self.cot[:, cols] = jnp.where(live, wide, 0.0).astype(jnp.bfloat16)

    def project(self, c):
        for cols in columns_of(self.width):
            wide = dot(self.attn[self.rows(c), :], self.weight[cols, :], (1, 1))
            self.projected[self.rows(c), cols] = wide.astype(jnp.bfloat16)

    def backward(self, c, first, past):
        rows = self.rows(c)
        inv_root = 1.0 / math.sqrt(self.head_dim)

        def head(h, carry):
            window, inside = self.window(h)
            key = self.key[rows, window]
            query = jnp.where(inside, self.query[rows, window], 0.0).astype(jnp.bfloat16)
            cot = jnp.where(inside, self.cot[:, window], 0.0).astype(jnp.bfloat16)
            weights = self.probs[h]

            def keep(target, found):
                found = found.astype(jnp.bfloat16)
                target[rows, window] = jnp.where(inside, found, target[rows, window])

            keep(self.grad_value, dot(weights.astype(jnp.bfloat16), cot, (1, 0)))
            grad_attn = dot(self.value[rows, window], cot, (1, 1))
            delta = jnp.sum(weights * grad_attn, axis=0, keepdims=True)
            grad_score = weights * (grad_attn - delta) * inv_root
            coarse = grad_score.astype(jnp.bfloat16)
            fine = (grad_score - coarse.astype(jnp.float32)).astype(jnp.bfloat16)
            keep(self.grad_query, dot(coarse, key, (0, 0)) + dot(fine, key, (0, 0)))
            keep(self.grad_key, dot(coarse, query, (1, 0)) + dot(fine, query, (1, 0)))
            return carry

        lax.fori_loop(first, past, head, 0)

    def weight_term(self, term, after):
        for cols in columns_of(self.width):
            found = dot(self.grad[:, cols], self.attn[...], (0, 0))
            for k in range(cols.size // 8):
                term[slab_place(cols.start // 8 + k)] = found[8 * k : 8 * k + 8]
            after(cols.start // 8, (cols.start + cols.size) // 8)


class Exchange:
    def __init__(self, n, clips, part, sems):
        self.n, self.clips, self.part = n, clips, part
        self.send, self.recv, self.local = sems
        self.me, self.rep = lax.axis_index("seq"), lax.axis_index("rep")

    def start(self, c, a, here, place, first, past):
        if first == 0:
            pltpu.make_async_copy(here(self.me), place, self.local.at[c, a]).start()

        def push(j, carry):
            peer = lax.rem(self.me + j, self.n)
            pltpu.make_async_remote_copy(
                src_ref=here(peer),
                dst_ref=place,
                send_sem=self.send.at[c, a],
                recv_sem=self.recv.at[c, a],
                device_id=(peer, self.rep),
                device_id_type=MESH,
            ).start()
            return carry

        lax.fori_loop(max(first, 1), past, push, 0)

    def tile(self, array, c, owner):
        return array.at[pl.ds(pl.multiple_of((c * self.n + owner) * self.part, self.part), self.part)]

    def strip(self, array, c, owner):
        return array.at[c, 0, pl.ds(pl.multiple_of(owner * self.part, self.part), self.part)]

    def bring(self, c, a, source, target):
        self.start(c, a, lambda peer: self.strip(source, c, peer), self.tile(target, c, self.me), 0, self.n)

    def give(self, c, a, source, target, first, past):
        place = self.strip(target, c, self.me)
        self.start(c, a, lambda peer: self.tile(source, c, peer), place, first, past)

    def wait(self, sem, count, array):
        some = array.at[pl.ds(0, count * self.part)]
        pltpu.make_async_copy(some, some, sem).wait()

    def arrived(self, c, a, array):
        self.wait(self.local.at[c, a], 1, array)
        self.wait(self.recv.at[c, a], self.n - 1, array)

    def left(self, c, a, array):
        self.wait(self.send.at[c, a], self.n - 1, array)


def fused_kernel(n, part, frames, places, *refs):
    sources, weight_hbm, targets, out = refs[:4], refs[4], refs[5:9], refs[9]
    arrived, results, scratch = refs[10:14], refs[14:18], refs[18:22]
    term, half, ring, plane, last, weight, weight_sem = refs[22:29]
    clips = sources[0].shape[0]
    inward, outward = Exchange(n, clips, part, refs[29:32]), Exchange(n, clips, part, refs[32:35])
    weight_sum = WeightSum(term, out, half, ring, plane, last, refs[35:])
    work = Attention(part, frames, places, weight, arrived, results, scratch)
    fetch = pltpu.make_async_copy(weight_hbm, weight, weight_sem)
    fetch.start()
    greet([row_peers(n)] + weight_sum.peers())
    for c in range(clips):
        for a in range(4):
            inward.bring(c, a, sources[a], arrived[a])

    ready = []

    def offer(c, arrays):
        ready.extend((c, a, first) for a in arrays for first in range(0, n, BATCH))

    def give(batches):
        for c, a, first in ready[:batches]:
            outward.give(c, a, results[a], targets[a], first, min(first + BATCH, n))
        del ready[:batches]

    end = clips - 1
    for c in range(clips):
        for a in range(3):
            inward.arrived(c, a, arrived[a])
        if c == end:
            give(4)
        work.forward(c)
        inward.arrived(c, 3, arrived[3])
        if c == 0:
            fetch.wait()
        if c < end:
            work.cotangent(c)
            work.backward(c, 0, HEADS)
            work.project(c)
            offer(c, range(4))
    give(8)
    work.weight_term(term, weight_sum.send_half)
    give(6)
    work.project(end)
    offer(end, [0])
    work.cotangent(end)
    weight_sum.add_half()
    weight_sum.ring_start()
    done = 0
    for t in range(RING - 1):
        for u in range(SLABS // SUB):
            if done < HEADS:
                work.backward(end, done, done + TOGETHER)
                done += TOGETHER
                if done == HEADS:
                    offer(end, range(1, 4))
            weight_sum.ring_step(t, u)
            give(1)
    weight_sum.spread(True)
    give(3)
    weight_sum.gather()
    give(len(ready))
    weight_sum.finish()
    for c in range(clips):
        for a in range(4):
            inward.left(c, a, arrived[a])
            outward.arrived(c, a, results[a])
            outward.left(c, a, results[a])


def fused(n, arrays, weight, frames, places):
    clips, _, all_places, width = arrays[0].shape
    part = all_places // n
    rows = n * part
    dma = pltpu.SemaphoreType.DMA
    smem, vmem, anywhere = (
        pl.BlockSpec(memory_space=space) for space in (pltpu.SMEM, pltpu.VMEM, pl.ANY)
    )
    return pl.pallas_call(
        functools.partial(fused_kernel, n, part),
        out_shape=[jax.ShapeDtypeStruct(arrays[0].shape, jnp.bfloat16)] * 4
        + [jax.ShapeDtypeStruct((SLABS * 8, width), jnp.float32)],
        in_specs=[smem, smem] + [anywhere] * 5,
        out_specs=[anywhere] * 4 + [vmem],
        scratch_shapes=[pltpu.VMEM((clips * rows, width), jnp.bfloat16)] * 8
        + [
            pltpu.VMEM((rows, width), jnp.bfloat16),
            pltpu.VMEM((clips * rows, width), jnp.bfloat16),
            pltpu.VMEM((rows, rows), jnp.float32),
            pltpu.VMEM((HEADS, rows, rows), jnp.float32),
            pltpu.VMEM((2, RING, SLABS, 8, width), jnp.float32),
            pltpu.VMEM((RING, SLABS, 8, width), jnp.float32),
            pltpu.VMEM((RING - 1, SLABS, 8, width), jnp.float32),
            pltpu.VMEM((2, 2 * RING, 8, 640), jnp.float32),
            pltpu.VMEM((2, 8, 640), jnp.float32),
            pltpu.VMEM((width, width), jnp.bfloat16),
            dma(()),
        ]
        + [dma((clips, 4))] * 6
        + [dma((2,)), dma((RING - 1, SLABS // SUB)), dma((RING - 1, SLABS // SUB)), dma((2, 2)), dma((3, 2))],
        compiler_params=pltpu.CompilerParams(
            collective_id=0, has_side_effects=True, vmem_limit_bytes=VMEM_BYTES
        ),
    )(frames, places, *arrays, weight)


def deliver_kernel(*refs):
    count = (len(refs) - 2) // 3
    sources, targets, held = refs[:count], refs[count : 2 * count], refs[2 * count : 3 * count]
    fetch = [pltpu.make_async_copy(sources[i], held[i], refs[-2].at[i]) for i in range(count)]
    store = [pltpu.make_async_copy(held[i], targets[i], refs[-1].at[i]) for i in range(count)]
    for copy in fetch:
        copy.start()
    for i in range(count):
        fetch[i].wait()
        store[i].start()
    for copy in store:
        copy.wait()


def deliver(arrays):
    count = len(arrays)
    return pl.pallas_call(
        deliver_kernel,
        out_shape=[jax.ShapeDtypeStruct(a.shape, a.dtype) for a in arrays],
        in_specs=[pl.BlockSpec(memory_space=pl.ANY)] * count,
        out_specs=[pl.BlockSpec(memory_space=pl.ANY)] * count,
        scratch_shapes=[pltpu.VMEM(a.shape, a.dtype) for a in arrays]
        + [pltpu.SemaphoreType.DMA((count,))] * 2,
        compiler_params=pltpu.CompilerParams(vmem_limit_bytes=VMEM_BYTES),
    )(*arrays)


def shards(query_rows, key_rows, value_rows, out_grad, out_weight, frame_count, pos_count):
    n = lax.axis_size("seq")
    arrays = (query_rows, key_rows, value_rows, out_grad)
    return tuple(deliver(fused(n, arrays, out_weight, frame_count, pos_count)))


def solution(mesh):
    rows = P("rep", "seq", None, None)
    return jax.shard_map(
        shards,
        mesh=mesh,
        in_specs=(rows, rows, rows, rows, P(), P("rep"), P("rep")),
        out_specs=(rows, rows, rows, rows, P("seq", None)),
        check_vma=False,
    )
```
